32 devices in a mesh: dom: 8 (over z, y), rows: 4 (over x, core).
Axes of the slice: x: 2, y: 2, z: 4, core: 2. Of those that a mesh axis runs over, the one named last changes fastest.
Arguments:
- images: bfloat16 [3584, 25600], P('dom', 'rows'), may hold values from -6 to 6
- panels: bfloat16 [16, 25600, 256], P('dom', 'rows')
- mean_panels: float32 [16, 25600], P('dom', 'rows'), may hold values from -6 to 6
- ctf_table: float32 [16, 25600], P(None, 'rows'), may hold values from -1 to 1
- pose_bin: int32 [3584], P('dom'), may hold values from 0 to 1
- ctf_group: int32 [3584], P('dom'), may hold values from 0 to 15
Outputs:
- scores: float32 [3584, 256], P('dom')
- factor: float32 [256, 256], replicated
The draws below stay inside these ranges and needn't reach their ends.
All inputs are finite; a program needn't handle non-finite values.
Results may differ from the reference program's by a relative error of at most 0.003.
Values sent between devices are 32-bit elements; how exact they have to be, the bound alone decides.
A program may use at most 128 MiB of HBM per device.

```python
import jax
import jax.numpy as jnp
from jax import lax

PROBES = 256
PART_DEV = 448
BIN_DEV = 2
GROUPS = 16
PIX = 25600
PARTICLES = 3584
BINS = 16
N_DOM = 8


def draw_panels(key, part):

    def one_bin(index):
        bin_key = jax.random.fold_in(key, index)
        key_common, key_single = jax.random.split(bin_key)
        common = jax.random.normal(key_common, (PIX, 1), jnp.float32)
        single = jax.random.normal(key_single, (PIX, PROBES + 2), jnp.float32)
        shared_weight = 0.6
        blended = shared_weight * common + single[:, 0:PROBES] + 0.8 * single[:, 1:PROBES + 1] + 0.5 * single[:, 2:PROBES + 2]
        spread = (1.89 + shared_weight * shared_weight) ** 0.5
        return blended * (1.0 / (spread * PIX ** 0.5))
    return lax.map(one_bin, jnp.arange(BINS, dtype=jnp.int32)).astype(jnp.bfloat16)


def plant(result, rng, smallest, top_value):
    longest = result.shape.index(max(result.shape))
    spots = []
    for shift in (0, 1):
        where = [jax.random.randint(jax.random.fold_in(rng, axis), (), 0, length) for axis, length in enumerate(result.shape)]
        where[longest] = (where[longest] + shift) % result.shape[longest]
        spots.append(tuple(where))
    return result.at[spots[0]].set(smallest).at[spots[1]].set(top_value)


def steps_of(rng, dims, cuts, least, top_value):
    def one(dim, shards_of):
        draws = jax.random.uniform(jax.random.fold_in(jax.random.fold_in(rng, 6), dim), (shards_of,), jnp.float32, least / len(cuts), top_value / len(cuts))
        return jnp.repeat(jnp.exp(draws), dims[dim] // shards_of).reshape((-1,) + (1,) * (len(dims) - dim - 1))

    gain = one(*cuts[0])
    for cut in cuts[1:]:
        gain = gain * one(*cut)
    return gain


def centred(stream_key, shape, scale, bound, cuts=(), kind=jnp.bfloat16):
    level = steps_of(stream_key, shape, cuts, -0.22, 0.18) if cuts else 1.0
    drawn = jax.random.normal(stream_key, shape, jnp.float32) * scale * level
    return jnp.minimum(jnp.maximum(drawn, -bound), bound).astype(kind)


def setup_inputs(seed: int = 0) -> dict:
    splits = jax.random.split(jax.random.key(seed), 7)
    return {
        "images": centred(splits[0], (PARTICLES, PIX), 1.0, 6.0, ((0, 8), (1, 4))),
        "panels": draw_panels(jax.random.fold_in(splits[6], 71), 0),
        "mean_panels": centred(splits[2], (BINS, PIX), 1.0, 6.0, ((0, 8), (1, 4)), jnp.float32),
        "ctf_table": jnp.clip(jax.random.uniform(splits[3], (GROUPS, PIX), jnp.float32, -1.0, 1.0) * steps_of(splits[3], (GROUPS, PIX), ((1, 4),), -0.4, 0.0), -1.0, 1.0),
        "pose_bin": plant(jax.random.randint(splits[4], (PARTICLES,), 0, BIN_DEV), jax.random.fold_in(splits[4], 1), 0, BIN_DEV - 1).astype(jnp.int32),
        "ctf_group": plant(jax.random.randint(splits[5], (PARTICLES,), 0, GROUPS), jax.random.fold_in(splits[5], 1), 0, GROUPS - 1).astype(jnp.int32),
    }


def high_dot(left, right):
    return jnp.dot(left, right, precision=lax.Precision.HIGHEST, preferred_element_type=jnp.float32)

def cholesky_small(matrix):
    order = matrix.shape[0]
    places = jnp.arange(order, dtype=jnp.int32)

    def column_step(index, carry):
        work, lower = carry
        index = jnp.asarray(index).astype(jnp.int32)
        column = lax.dynamic_slice_in_dim(work, index, 1, 1)[:, 0]
        pivot = jnp.sqrt(lax.dynamic_slice_in_dim(column, index, 1, 0)[0])
        below = jnp.where(places > index, column / pivot, jnp.zeros_like(column))
        filled = below + jnp.where(places == index, pivot, jnp.zeros_like(column))
        lower = lower + filled[:, None] * (places == index).astype(matrix.dtype)[None, :]
        work = work - below[:, None] * below[None, :]
        return (work, lower)
    return lax.fori_loop(0, order, column_step, (matrix, jnp.zeros_like(matrix)))[1]

def inverse_small(lower):
    order = lower.shape[0]
    places = jnp.arange(order, dtype=jnp.int32)

    def row_step(index, inverse):
        index = jnp.asarray(index).astype(jnp.int32)
        row_lower = lax.dynamic_slice_in_dim(lower, index, 1, 0)[0]
        pivot = lax.dynamic_slice_in_dim(row_lower, index, 1, 0)[0]
        unit = (places == index).astype(lower.dtype)
        solved = (unit - high_dot(row_lower, inverse)) / pivot
        return inverse + unit[:, None] * solved[None, :]
    return lax.fori_loop(0, order, row_step, jnp.zeros_like(lower))

def assemble(top_left, bottom_left, bottom_right):
    half = top_left.shape[0]
    rest = bottom_right.shape[0]
    upper_part = jnp.concatenate([top_left, jnp.zeros((half, rest), top_left.dtype)], axis=1)
    lower_part = jnp.concatenate([bottom_left, bottom_right], axis=1)
    return jnp.concatenate([upper_part, lower_part], axis=0)

def cholesky_pair(matrix):
    order = matrix.shape[0]
    if order <= 16:
        lower = cholesky_small(matrix)
        return (lower, inverse_small(lower))
    half = order // 2
    lower_a, inverse_a = cholesky_pair(matrix[:half, :half])
    below = high_dot(matrix[half:, :half], inverse_a.T)
    schur = matrix[half:, half:] - high_dot(below, below.T)
    lower_b, inverse_b = cholesky_pair(schur)
    inverse_mid = -high_dot(inverse_b, high_dot(below, inverse_a))
    return (assemble(lower_a, below, lower_b), assemble(inverse_a, inverse_mid, inverse_b))

def lower_inverse(lower):
    order = lower.shape[0]
    if order <= 16:
        return inverse_small(lower)
    half = order // 2
    inverse_a = lower_inverse(lower[:half, :half])
    inverse_b = lower_inverse(lower[half:, half:])
    inverse_mid = -high_dot(inverse_b, high_dot(lower[half:, :half], inverse_a))
    return assemble(inverse_a, inverse_mid, inverse_b)

def weighted_block(images_block, pose_block, group_block, panel_block, mean_block, ctf_table):
    ctf_rows = jnp.take(ctf_table, group_block.astype(jnp.int32), axis=0)
    mean_rows = jnp.take(mean_block, pose_block.astype(jnp.int32), axis=0)
    weighted = (ctf_rows * (images_block.astype(jnp.float32) - ctf_rows * mean_rows)).astype(jnp.bfloat16)
    coeffs = jnp.zeros((images_block.shape[0], panel_block.shape[2]), jnp.float32)
    for which in range(BIN_DEV):
        chosen = jnp.where((pose_block == which)[:, None], weighted, jnp.zeros_like(weighted))
        coeffs = coeffs + jnp.dot(chosen, panel_block[which], preferred_element_type=jnp.float32)
    return coeffs

def reference(images, panels, mean_panels, ctf_table, pose_bin, ctf_group):
    images_r = images.reshape(N_DOM, PART_DEV, PIX)
    pose_r = pose_bin.reshape(N_DOM, PART_DEV)
    group_r = ctf_group.reshape(N_DOM, PART_DEV)
    panels_r = panels.reshape(N_DOM, BIN_DEV, PIX, PROBES)
    means_r = mean_panels.reshape(N_DOM, BIN_DEV, PIX)

    def one_block(pieces):
        return weighted_block(pieces[0], pieces[1], pieces[2], pieces[3], pieces[4], ctf_table)
    coeffs = lax.map(one_block, (images_r, pose_r, group_r, panels_r, means_r)).reshape(PARTICLES, PROBES)
    gram = high_dot(coeffs.T, coeffs) / PARTICLES
    lower, inverse = cholesky_pair(gram)
    scores = jnp.dot(coeffs, inverse.T, precision=lax.Precision.HIGHEST)
    return (scores, lower.T)
```

```python
import functools

import jax
import jax.numpy as jnp
from jax import lax
from jax.experimental import pallas as pl
from jax.experimental.pallas import tpu as pltpu
from jax.sharding import PartitionSpec as P

F32 = jnp.float32
BF16 = jnp.bfloat16


def dot_f32(left, right, dims):
    return lax.dot_general(
        left, right, (dims, ((), ())), precision=lax.Precision.HIGHEST, preferred_element_type=F32
    )


def widen(column, lanes):
    return jnp.concatenate([column] * (lanes // 128), axis=1)


def project_kernel(groups, steps, images, panels, means, table, pose, group, out, pick, mask, acc):
    step = pl.program_id(0)
    rows, chunk = images.shape

    @pl.when(step == 0)
    def _():
        place = lax.broadcasted_iota(jnp.int32, (128, rows), 0)
        hot = (place % groups == group[...]) & (place < 3 * groups)
        pick[...] = jnp.transpose(hot.astype(F32)).astype(BF16)
        mask[...] = jnp.transpose(jnp.broadcast_to(pose[...].astype(F32), (128, rows)))
        acc[...] = jnp.zeros_like(acc)

    exact = table[...]
    high = exact.astype(BF16)
    left = exact - high.astype(F32)
    mid = left.astype(BF16)
    low = (left - mid.astype(F32)).astype(BF16)
    fill = jnp.zeros((128 - 3 * groups, chunk), BF16)
    parts = jnp.concatenate([high, mid, low, fill], axis=0)
    ctf = jnp.dot(pick[...], parts, preferred_element_type=F32)
    second = widen(mask[...], chunk) > 0.5
    mean = jnp.where(second, means[1:2, :], means[0:1, :])
    weighted = (ctf * (images[...].astype(F32) - ctf * mean)).astype(BF16)
    for which in range(2):
        acc[which] += jnp.dot(weighted, panels[which], preferred_element_type=F32)

    @pl.when(step == steps - 1)
    def _():
        out[...] = jnp.where(widen(mask[...], out.shape[1]) > 0.5, acc[1], acc[0])


def project(images, panels, means, table, pose, group):
    rows, pixels = images.shape
    bins, _, probes = panels.shape
    groups = table.shape[0]
    chunk = 1280 if pixels % 1280 == 0 else 128
    steps = pixels // chunk
    return pl.pallas_call(
        functools.partial(project_kernel, groups, steps),
        grid=(steps,),
        in_specs=[
            pl.BlockSpec((rows, chunk), lambda i: (0, i)),
            pl.BlockSpec((bins, chunk, probes), lambda i: (0, i, 0)),
            pl.BlockSpec((bins, chunk), lambda i: (0, i)),
            pl.BlockSpec((groups, chunk), lambda i: (0, i)),
            pl.BlockSpec((1, rows), lambda i: (0, 0)),
            pl.BlockSpec((1, rows), lambda i: (0, 0)),
        ],
        out_specs=pl.BlockSpec((rows, probes), lambda i: (0, 0)),
        out_shape=jax.ShapeDtypeStruct((rows, probes), F32),
        scratch_shapes=[
            pltpu.VMEM((rows, 128), BF16),
            pltpu.VMEM((rows, 128), F32),
            pltpu.VMEM((bins, rows, probes), F32),
        ],
        compiler_params=pltpu.CompilerParams(vmem_limit_bytes=60 * 2**20),
        name="project",
    )(images, panels, means, table, pose.reshape(1, rows), group.reshape(1, rows))


SIZE = 64
PANEL = 4


def factor_block(block):
    lane = lax.broadcasted_iota(jnp.int32, (8, 2 * SIZE), 1)
    sub = lax.broadcasted_iota(jnp.int32, (8, 2 * SIZE), 0)
    tiles = []
    for t in range(SIZE // 8):
        unit = (lane == sub + (8 * t + SIZE)).astype(F32)
        part = jnp.concatenate([block[8 * t : 8 * t + 8], jnp.zeros((8, SIZE), F32)], axis=1)
        tiles.append(part + unit)
    count = len(tiles)
    pivots = [jnp.ones((8, 2 * SIZE), F32) for _ in range(count)]
    for base in range(0, SIZE, PANEL):
        first = base // 8
        cols = [
            [None] * first
            + [jnp.broadcast_to(tiles[t][:, base + j : base + j + 1], (8, 2 * SIZE)) for t in range(first, count)]
            for j in range(PANEL)
        ]
        for j in range(PANEL):
            k = base + j
            row = k % 8
            pivot = cols[j][first][row : row + 1]
            inverse = 1.0 / pivot
            pivots[first] = jnp.where(sub == row, pivot, pivots[first])
            scale = [None] * count
            for t in range(first, count):
                scale[t] = cols[j][t] * inverse
            scale[first] = jnp.where(sub > row, scale[first], 0.0)
            for later in range(j + 1, PANEL):
                value = cols[later][first][row : row + 1]
                for t in range(first, count):
                    cols[later][t] = cols[later][t] - scale[t] * value
            line = tiles[first][row : row + 1]
            for t in range(first, count):
                tiles[t] = tiles[t] - scale[t] * line
    done = []
    for t in range(count):
        keep = (lane >= SIZE) | (lane >= sub + 8 * t)
        done.append(jnp.where(keep, tiles[t] * lax.rsqrt(pivots[t]), 0.0))
    return jnp.concatenate(done, axis=0)


def finish_kernel(particles, gram, coeffs, scores, factor, work, side):
    order = gram.shape[0]
    work[...] = gram[...] * (1.0 / particles)
    spot = lax.broadcasted_iota(jnp.int32, (order, order), 0)
    side[...] = (spot == lax.broadcasted_iota(jnp.int32, (order, order), 1)).astype(F32)
    for start in range(0, order, SIZE):
        stop = start + SIZE
        both = factor_block(work[start:stop, start:stop])
        upper, lower = both[:, :SIZE], both[:, SIZE:]
        if start:
            factor[start:stop, :start] = jnp.zeros((SIZE, start), F32)
        factor[start:stop, start:stop] = upper
        reach = -(-stop // 128) * 128
        row_side = dot_f32(lower, side[start:stop, :reach], ((1,), (0,)))
        side[start:stop, :reach] = row_side
        if stop < order:
            from_col = stop // 128 * 128
            row_work = dot_f32(lower, work[start:stop, from_col:], ((1,), (0,)))
            right = row_work[:, stop - from_col :]
            factor[start:stop, stop:] = right
            work[stop:, from_col:] = work[stop:, from_col:] - dot_f32(right, row_work, ((0,), (0,)))
            side[stop:, :reach] = side[stop:, :reach] - dot_f32(right, row_side, ((0,), (0,)))
    scores[...] = dot_f32(coeffs[...], side[...], ((1,), (1,)))


def finish(gram, coeffs, particles):
    order = gram.shape[0]
    return pl.pallas_call(
        functools.partial(finish_kernel, particles),
        in_specs=[pl.BlockSpec(memory_space=pltpu.VMEM)] * 2,
        out_specs=[pl.BlockSpec(memory_space=pltpu.VMEM)] * 2,
        out_shape=[jax.ShapeDtypeStruct(coeffs.shape, F32), jax.ShapeDtypeStruct((order, order), F32)],
        scratch_shapes=[pltpu.VMEM((order, order), F32)] * 2,
        name="finish",
    )(gram, coeffs)


MESH = pl.DeviceIdType.MESH
CHUNKS = 4


def combine_kernel(n_rows, n_dom, part, coeffs, gram, near, far, held, wide, give, take, *sems):
    pair_send, pair_recv, far_send, far_recv, back_send, back_recv = sems[:6]
    dom_send, dom_recv, all_send, all_recv, row_send, row_recv = sems[6:]
    row, dom = lax.axis_index("rows"), lax.axis_index("dom")
    side, pair = row % 2, row // 2
    other = 1 - side
    partner = pair * 2 + other
    across = (1 - pair) * 2 + side
    half = part.shape[0] // 2
    size = half // CHUNKS
    order = part.shape[1]
    slab = order // n_rows
    piece = slab // n_dom

    def to(source, target, send, recv, place):
        return pltpu.make_async_remote_copy(
            src_ref=source, dst_ref=target, send_sem=send, recv_sem=recv, device_id=place, device_id_type=MESH
        )

    barrier = pltpu.get_barrier_semaphore()
    for step in range(1, n_rows):
        pl.semaphore_signal(barrier, inc=1, device_id=(dom, (row + step) % n_rows), device_id_type=MESH)
    for step in range(1, n_dom):
        pl.semaphore_signal(barrier, inc=1, device_id=((dom + step) % n_dom, row), device_id_type=MESH)
    pl.semaphore_wait(barrier, n_rows + n_dom - 2)

    def mine(start, chunk):
        return pl.ds(pl.multiple_of(start * half + chunk * size, 8), size)

    first = []
    for c in range(CHUNKS):
        first.append(
            to(part.at[mine(other, c)], near.at[c], pair_send.at[c], pair_recv.at[c], (dom, partner))
        )
        first[c].start()
    second = []
    for c in range(CHUNKS):
        first[c].wait_recv()
        held[c] = part[mine(side, c), :] + near[c]
        second.append(to(held.at[c], far.at[c], far_send.at[c], far_recv.at[c], (dom, across)))
        second[c].start()
    third = []
    for c in range(CHUNKS):
        second[c].wait_recv()
        coeffs[mine(side, c), :] = held[c] + far[c]
        ours = coeffs.at[mine(side, c)]
        third.append(to(ours, ours, back_send.at[c], back_recv.at[c], (dom, partner)))
        third[c].start()

    span = max(slab, 128)
    columns = pl.ds(pl.multiple_of(row * slab // span * span, 128), span)

    def square(start):
        rows = pl.ds(pl.multiple_of(start * half, 8), half)
        return dot_f32(coeffs[rows, columns], coeffs[rows, :], ((0,), (0,)))

    wide[...] = square(side)
    for c in range(CHUNKS):
        third[c].wait_recv()
    wide[...] = wide[...] + square(other)
    ours = wide[pl.ds(pl.multiple_of(row * slab % span, 8), slab), :]
    for d in range(n_dom):
        give[d] = ours[d * piece : (d + 1) * piece, :]

    out = []
    for step in range(1, n_dom):
        there = (dom + step) % n_dom
        out.append(
            to(give.at[there], take.at[dom], dom_send.at[step - 1], dom_recv.at[step - 1], (there, row))
        )
        out[-1].start()
    take[dom] = give[dom]
    for copy in out:
        copy.wait_recv()
    total = take[0]
    for d in range(1, n_dom):
        total = total + take[d]
    gram[row, dom] = total

    spread = []
    for step in range(1, n_dom):
        there = (dom + step) % n_dom
        block = gram.at[row, dom]
        spread.append(to(block, block, all_send.at[step - 1], all_recv.at[step - 1], (there, row)))
        spread[-1].start()
    for copy in spread:
        copy.wait_recv()
    last = []
    for step in range(1, n_rows):
        there = (row + step) % n_rows
        block = gram.at[row]
        last.append(to(block, block, row_send.at[step - 1], row_recv.at[step - 1], (dom, there)))
        last[-1].start()
    for copy in last:
        copy.wait_recv()
    for copy in first + second + third + out + spread + last:
        copy.wait_send()


def combine(part):
    n_rows, n_dom = lax.axis_size("rows"), lax.axis_size("dom")
    count, order = part.shape
    slab = order // n_rows
    piece = slab // n_dom
    size = count // 2 // CHUNKS
    dma = pltpu.SemaphoreType.DMA
    coeffs, gram = pl.pallas_call(
        functools.partial(combine_kernel, n_rows, n_dom),
        in_specs=[pl.BlockSpec(memory_space=pltpu.VMEM)],
        out_specs=[pl.BlockSpec(memory_space=pltpu.VMEM)] * 2,
        out_shape=[
            jax.ShapeDtypeStruct((count, order), F32),
            jax.ShapeDtypeStruct((n_rows, n_dom, piece, order), F32),
        ],
        scratch_shapes=[
            pltpu.VMEM((CHUNKS, size, order), F32),
            pltpu.VMEM((CHUNKS, size, order), F32),
            pltpu.VMEM((CHUNKS, size, order), F32),
            pltpu.VMEM((max(slab, 128), order), F32),
            pltpu.VMEM((n_dom, piece, order), F32),
            pltpu.VMEM((n_dom, piece, order), F32),
        ]
        + [dma((CHUNKS,))] * 6
        + [dma((n_dom - 1,))] * 4
        + [dma((n_rows - 1,))] * 2,
        compiler_params=pltpu.CompilerParams(collective_id=0, has_side_effects=True),
        name="combine",
    )(part)
    return coeffs, gram.reshape(order, order)


def body(images, panels, mean_panels, ctf_table, pose_bin, ctf_group):
    particles = images.shape[0] * lax.axis_size("dom")
    coeffs, gram = combine(project(images, panels, mean_panels, ctf_table, pose_bin, ctf_group))
    return tuple(finish(gram, coeffs, particles))


def solution(mesh):
    placed = (
        P("dom", "rows"),
        P("dom", "rows", None),
        P("dom", "rows"),
        P(None, "rows"),
        P("dom"),
        P("dom"),
    )
    return jax.shard_map(
        body, mesh=mesh, in_specs=placed, out_specs=(P("dom", None), P()), check_vma=False
    )
```

```python
import functools

import jax
import jax.numpy as jnp
from jax import lax
from jax.experimental import pallas as pl
from jax.experimental.pallas import tpu as pltpu
from jax.sharding import PartitionSpec as P

F32 = jnp.float32
BF16 = jnp.bfloat16


def dot_f32(left, right, dims):
    return lax.dot_general(
        left, right, (dims, ((), ())), precision=lax.Precision.HIGHEST, preferred_element_type=F32
    )


def widen(column, lanes):
    return jnp.concatenate([column] * (lanes // 128), axis=1)


def project_kernel(groups, steps, images, panels, means, table, pose, group, out, pick, mask, acc):
    step = pl.program_id(0)
    rows, chunk = images.shape

    @pl.when(step == 0)
    def _():
        place = lax.broadcasted_iota(jnp.int32, (128, rows), 0)
        hot = (place % groups == group[...]) & (place < 3 * groups)
        pick[...] = jnp.transpose(hot.astype(F32)).astype(BF16)
        mask[...] = jnp.transpose(jnp.broadcast_to(pose[...].astype(F32), (128, rows)))
        acc[...] = jnp.zeros_like(acc)

    exact = table[...]
    high = exact.astype(BF16)
    left = exact - high.astype(F32)
    mid = left.astype(BF16)
    low = (left - mid.astype(F32)).astype(BF16)
    fill = jnp.zeros((128 - 3 * groups, chunk), BF16)
    parts = jnp.concatenate([high, mid, low, fill], axis=0)
    ctf = jnp.dot(pick[...], parts, preferred_element_type=F32)
    second = widen(mask[...], chunk) > 0.5
    mean = jnp.where(second, means[1:2, :], means[0:1, :])
    weighted = (ctf * (images[...].astype(F32) - ctf * mean)).astype(BF16)
    for which in range(2):
        acc[which] += jnp.dot(weighted, panels[which], preferred_element_type=F32)

    @pl.when(step == steps - 1)
    def _():
        out[...] = jnp.where(widen(mask[...], out.shape[1]) > 0.5, acc[1], acc[0])


def project(images, panels, means, table, pose, group):
    rows, pixels = images.shape
    bins, _, probes = panels.shape
    groups = table.shape[0]
    chunk = 1280 if pixels % 1280 == 0 else 128
    steps = pixels // chunk
    return pl.pallas_call(
        functools.partial(project_kernel, groups, steps),
        grid=(steps,),
        in_specs=[
            pl.BlockSpec((rows, chunk), lambda i: (0, i)),
            pl.BlockSpec((bins, chunk, probes), lambda i: (0, i, 0)),
            pl.BlockSpec((bins, chunk), lambda i: (0, i)),
            pl.BlockSpec((groups, chunk), lambda i: (0, i)),
            pl.BlockSpec((1, rows), lambda i: (0, 0)),
            pl.BlockSpec((1, rows), lambda i: (0, 0)),
        ],
        out_specs=pl.BlockSpec((rows, probes), lambda i: (0, 0)),
        out_shape=jax.ShapeDtypeStruct((rows, probes), F32),
        scratch_shapes=[
            pltpu.VMEM((rows, 128), BF16),
            pltpu.VMEM((rows, 128), F32),
            pltpu.VMEM((bins, rows, probes), F32),
        ],
        compiler_params=pltpu.CompilerParams(vmem_limit_bytes=60 * 2**20),
        name="project",
    )(images, panels, means, table, pose.reshape(1, rows), group.reshape(1, rows))


SIZE = 64
PANEL = 16


def factor_block(block):
    lane = lax.broadcasted_iota(jnp.int32, (8, 2 * SIZE), 1)
    sub = lax.broadcasted_iota(jnp.int32, (8, 2 * SIZE), 0)
    tiles = []
    for t in range(SIZE // 8):
        unit = (lane == sub + (8 * t + SIZE)).astype(F32)
        part = jnp.concatenate([block[8 * t : 8 * t + 8], jnp.zeros((8, SIZE), F32)], axis=1)
        tiles.append(part + unit)
    count = len(tiles)
    pivots = [jnp.ones((8, 2 * SIZE), F32) for _ in range(count)]
    for base in range(0, SIZE, PANEL):
        first = base // 8
        cols = [
            [None] * first
            + [jnp.broadcast_to(tiles[t][:, base + j : base + j + 1], (8, 2 * SIZE)) for t in range(first, count)]
            for j in range(PANEL)
        ]
        for j in range(PANEL):
            k = base + j
            row, here = k % 8, k // 8
            pivot = cols[j][here][row : row + 1]
            inverse = 1.0 / pivot
            pivots[here] = jnp.where(sub == row, pivot, pivots[here])
            scale = [None] * count
            for t in range(here, count):
                scale[t] = cols[j][t] * inverse
            scale[here] = jnp.where(sub > row, scale[here], 0.0)
            for later in range(j + 1, PANEL):
                value = cols[later][here][row : row + 1]
                for t in range(here, count):
                    cols[later][t] = cols[later][t] - scale[t] * value
            line = tiles[here][row : row + 1]
            for t in range(here, count):
                tiles[t] = tiles[t] - scale[t] * line
    done = []
    for t in range(count):
        keep = (lane >= SIZE) | (lane >= sub + 8 * t)
        done.append(jnp.where(keep, tiles[t] * lax.rsqrt(pivots[t]), 0.0))
    return jnp.concatenate(done, axis=0)


def finish_kernel(particles, gram, coeffs, scores, factor, work, side):
    order = gram.shape[0]
    work[...] = gram[...] * (1.0 / particles)
    spot = lax.broadcasted_iota(jnp.int32, (order, order), 0)
    side[...] = (spot == lax.broadcasted_iota(jnp.int32, (order, order), 1)).astype(F32)
    for start in range(0, order, SIZE):
        stop = start + SIZE
        both = factor_block(work[start:stop, start:stop])
        upper, lower = both[:, :SIZE], both[:, SIZE:]
        if start:
            factor[start:stop, :start] = jnp.zeros((SIZE, start), F32)
        factor[start:stop, start:stop] = upper
        reach = -(-stop // 128) * 128
        row_side = dot_f32(lower, side[start:stop, :reach], ((1,), (0,)))
        side[start:stop, :reach] = row_side
        if stop < order:
            from_col = stop // 128 * 128
            row_work = dot_f32(lower, work[start:stop, from_col:], ((1,), (0,)))
            right = row_work[:, stop - from_col :]
            factor[start:stop, stop:] = right
            work[stop:, from_col:] = work[stop:, from_col:] - dot_f32(right, row_work, ((0,), (0,)))
            side[stop:, :reach] = side[stop:, :reach] - dot_f32(right, row_side, ((0,), (0,)))
    scores[...] = dot_f32(coeffs[...], side[...], ((1,), (1,)))


def finish(gram, coeffs, particles):
    order = gram.shape[0]
    return pl.pallas_call(
        functools.partial(finish_kernel, particles),
        in_specs=[pl.BlockSpec(memory_space=pltpu.VMEM)] * 2,
        out_specs=[pl.BlockSpec(memory_space=pltpu.VMEM)] * 2,
        out_shape=[jax.ShapeDtypeStruct(coeffs.shape, F32), jax.ShapeDtypeStruct((order, order), F32)],
        scratch_shapes=[pltpu.VMEM((order, order), F32)] * 2,
        name="finish",
    )(gram, coeffs)


MESH = pl.DeviceIdType.MESH
CHUNKS = 4


def combine_kernel(n_rows, n_dom, part, coeffs, gram, near, far, held, wide, give, take, *sems):
    pair_send, pair_recv, far_send, far_recv, back_send, back_recv = sems[:6]
    dom_send, dom_recv, all_send, all_recv, row_send, row_recv = sems[6:]
    row, dom = lax.axis_index("rows"), lax.axis_index("dom")
    side, pair = row % 2, row // 2
    other = 1 - side
    partner = pair * 2 + other
    across = (1 - pair) * 2 + side
    half = part.shape[0] // 2
    size = half // CHUNKS
    order = part.shape[1]
    slab = order // n_rows
    piece = slab // n_dom

    def to(source, target, send, recv, place):
        return pltpu.make_async_remote_copy(
            src_ref=source, dst_ref=target, send_sem=send, recv_sem=recv, device_id=place, device_id_type=MESH
        )

    barrier = pltpu.get_barrier_semaphore()
    for step in range(1, n_rows):
        pl.semaphore_signal(barrier, inc=1, device_id=(dom, (row + step) % n_rows), device_id_type=MESH)
    for step in range(1, n_dom):
        pl.semaphore_signal(barrier, inc=1, device_id=((dom + step) % n_dom, row), device_id_type=MESH)
    pl.semaphore_wait(barrier, n_rows + n_dom - 2)

    def mine(start, chunk):
        return pl.ds(pl.multiple_of(start * half + chunk * size, 8), size)

    first = []
    for c in range(CHUNKS):
        first.append(
            to(part.at[mine(other, c)], near.at[c], pair_send.at[c], pair_recv.at[c], (dom, partner))
        )
        first[c].start()
    second = []
    for c in range(CHUNKS):
        first[c].wait_recv()
        held[c] = part[mine(side, c), :] + near[c]
        second.append(to(held.at[c], far.at[c], far_send.at[c], far_recv.at[c], (dom, across)))
        second[c].start()
    third = []
    for c in range(CHUNKS):
        second[c].wait_recv()
        coeffs[mine(side, c), :] = held[c] + far[c]
        ours = coeffs.at[mine(side, c)]
        third.append(to(ours, ours, back_send.at[c], back_recv.at[c], (dom, partner)))
        third[c].start()

    span = max(slab, 128)
    columns = pl.ds(pl.multiple_of(row * slab // span * span, 128), span)

    def square(start):
        rows = pl.ds(pl.multiple_of(start * half, 8), half)
        return dot_f32(coeffs[rows, columns], coeffs[rows, :], ((0,), (0,)))

    wide[...] = square(side)
    for c in range(CHUNKS):
        third[c].wait_recv()
    wide[...] = wide[...] + square(other)
    ours = wide[pl.ds(pl.multiple_of(row * slab % span, 8), slab), :]
    for d in range(n_dom):
        give[d] = ours[d * piece : (d + 1) * piece, :]

    out = []
    for step in range(1, n_dom):
        there = (dom + step) % n_dom
        out.append(
            to(give.at[there], take.at[dom], dom_send.at[step - 1], dom_recv.at[step - 1], (there, row))
        )
        out[-1].start()
    take[dom] = give[dom]
    for copy in out:
        copy.wait_recv()
    total = take[0]
    for d in range(1, n_dom):
        total = total + take[d]
    gram[row, dom] = total

    def relay(owner, slot):
        block = gram.at[row, owner]
        for step in range(1, n_rows):
            there = (row + step) % n_rows
            place = (step - 1, slot)
            last.append(to(block, block, row_send.at[place], row_recv.at[place], (dom, there)))
            last[-1].start()

    spread, last = [], []
    for step in range(1, n_dom):
        there = (dom + step) % n_dom
        block = gram.at[row, dom]
        spread.append(to(block, block, all_send.at[step - 1], all_recv.at[step - 1], (there, row)))
        spread[-1].start()
    relay(dom, 0)
    for step in range(1, n_dom):
        spread[step - 1].wait_recv()
        relay((dom - step + n_dom) % n_dom, step)
    for copy in last:
        copy.wait_recv()
    for copy in first + second + third + out + spread + last:
        copy.wait_send()


def combine(part):
    n_rows, n_dom = lax.axis_size("rows"), lax.axis_size("dom")
    count, order = part.shape
    slab = order // n_rows
    piece = slab // n_dom
    size = count // 2 // CHUNKS
    dma = pltpu.SemaphoreType.DMA
    coeffs, gram = pl.pallas_call(
        functools.partial(combine_kernel, n_rows, n_dom),
        in_specs=[pl.BlockSpec(memory_space=pltpu.VMEM)],
        out_specs=[pl.BlockSpec(memory_space=pltpu.VMEM)] * 2,
        out_shape=[
            jax.ShapeDtypeStruct((count, order), F32),
            jax.ShapeDtypeStruct((n_rows, n_dom, piece, order), F32),
        ],
        scratch_shapes=[
            pltpu.VMEM((CHUNKS, size, order), F32),
            pltpu.VMEM((CHUNKS, size, order), F32),
            pltpu.VMEM((CHUNKS, size, order), F32),
            pltpu.VMEM((max(slab, 128), order), F32),
            pltpu.VMEM((n_dom, piece, order), F32),
            pltpu.VMEM((n_dom, piece, order), F32),
        ]
        + [dma((CHUNKS,))] * 6
        + [dma((n_dom - 1,))] * 4
        + [dma((n_rows - 1, n_dom))] * 2,
        compiler_params=pltpu.CompilerParams(collective_id=0, has_side_effects=True),
        name="combine",
    )(part)
    return coeffs, gram.reshape(order, order)


def body(images, panels, mean_panels, ctf_table, pose_bin, ctf_group):
    particles = images.shape[0] * lax.axis_size("dom")
    coeffs, gram = combine(project(images, panels, mean_panels, ctf_table, pose_bin, ctf_group))
    return tuple(finish(gram, coeffs, particles))


def solution(mesh):
    placed = (
        P("dom", "rows"),
        P("dom", "rows", None),
        P("dom", "rows"),
        P(None, "rows"),
        P("dom"),
        P("dom"),
    )
    return jax.shard_map(
        body, mesh=mesh, in_specs=placed, out_specs=(P("dom", None), P()), check_vma=False
    )
```
